32 devices in a mesh: gz: 16 (over z, y, x), gy: 2 (over core).
Axes of the slice: x: 2, y: 2, z: 4, core: 2. Of those that a mesh axis runs over, the one named last changes fastest.
Arguments:
- velocity: bfloat16 [3, 128, 128, 128], P(None, 'gz', 'gy'), may hold values from -6 to 6
- palette_color: float32 [3, 64], replicated, may hold values from 0 to 1
- palette_extinction: float32 [64], replicated, may hold values from 0.0003 to 0.02
- palette_index: int32 [16], replicated, may hold values from 0 to 63
Outputs:
- image: float32 [4, 2, 64, 128], P(None, 'gy', 'gz')
The draws below stay inside these ranges and needn't reach their ends.
All inputs are finite; a program needn't handle non-finite values.
Results may differ from the reference program's by a relative error of at most 0.0012.
Values may be sent and summed in bfloat16 or wider, within the bound.
A program may use at most 64 MiB of HBM per device.

```python
import math
import jax
import jax.numpy as jnp
from jax import lax

NX = 128
CY = 64
RADIUS = 4
TF_POINTS = 16
PALETTE = 64
NY = 128
NZ = 128
N_GY = 2


def touch_ends(entries, own_key, least, top_value):
    longest = entries.shape.index(max(entries.shape))
    spots = []
    for shift in (0, 1):
        where = [jax.random.randint(jax.random.fold_in(own_key, axis), (), 0, length) for axis, length in enumerate(entries.shape)]
        where[longest] = (where[longest] + shift) % entries.shape[longest]
        spots.append(tuple(where))
    return entries.at[spots[0]].set(least).at[spots[1]].set(top_value)


def levels(key, extent, split, least, high):
    factor_of, own = 1.0, jax.random.fold_in(key, 6)
    for dim, blocks in split:
        steps = jnp.exp(jax.random.uniform(jax.random.fold_in(own, dim), (blocks,), jnp.float32, least / len(split), high / len(split)))
        factor_of = factor_of * jnp.repeat(steps, extent[dim] // blocks).reshape([-1 if axis == dim else 1 for axis in range(len(extent))])
    return factor_of


def centred(rng, shape, width, reach, pieces=(), held_as=jnp.bfloat16):
    array = jax.random.normal(rng, shape, jnp.float32) * width
    if len(pieces) > 0:
        array = levels(rng, shape, pieces, -0.22, 0.18) * array
    return jnp.clip(array, min=-reach, max=reach).astype(held_as)


def setup_inputs(seed: int = 0) -> dict:
    streams_of = jax.random.split(jax.random.key(seed), 5)
    return {
        "velocity": centred(streams_of[0], (3, NZ, NY, NX), 1.0, 6.0, ((1, 16), (2, 2))),
        "palette_color": jnp.clip(jax.random.uniform(streams_of[1], (3, PALETTE), jnp.float32, 0.0, 1.0), 0.0, 1.0),
        "palette_extinction": jnp.clip(jnp.exp(jax.random.uniform(streams_of[2], (PALETTE,), jnp.float32, math.log(0.0003), math.log(0.02))), 0.0003, 0.02),
        "palette_index": touch_ends(jax.random.randint(streams_of[3], (TF_POINTS,), 0, PALETTE), jax.random.fold_in(streams_of[3], 1), 0, PALETTE - 1).astype(jnp.int32),
    }


filter_sigma = 1.5
vortex_gain = 400.0


def filter_taps():
    weights = [math.exp(-((offset - RADIUS) ** 2) / (2.0 * filter_sigma ** 2)) for offset in range(2 * RADIUS + 1)]
    weight_sum = sum(weights)
    gauss = [weight / weight_sum for weight in weights]
    moment = sum(((offset - RADIUS) ** 2) * gauss[offset] for offset in range(2 * RADIUS + 1))
    deriv = [(offset - RADIUS) * gauss[offset] / moment for offset in range(2 * RADIUS + 1)]
    return gauss, deriv


def smooth_along(field, taps, dimension):
    span = field.shape[dimension] - 2 * RADIUS
    result = taps[0] * lax.slice_in_dim(field, 0, span, axis=dimension)
    for offset in range(1, 2 * RADIUS + 1):
        result = result + taps[offset] * lax.slice_in_dim(field, offset, offset + span, axis=dimension)
    return result


def vortex_measure(grad_x, grad_y, grad_z):
    grads = [[grad_x[comp], grad_y[comp], grad_z[comp]] for comp in range(3)]
    total = jnp.zeros_like(grad_x[0])
    for first in range(3):
        for second in range(3):
            total = total + grads[first][second] * grads[second][first]
    return -0.5 * total


def lookup_tables(palette_color, palette_extinction, palette_index):
    onehot = (palette_index[:, None] == jnp.arange(PALETTE, dtype=jnp.int32)[None, :]).astype(jnp.float32)
    color_table = jnp.dot(palette_color, onehot.T, precision=lax.Precision.HIGHEST, preferred_element_type=jnp.float32)
    extinction_table = jnp.dot(onehot, palette_extinction, precision=lax.Precision.HIGHEST, preferred_element_type=jnp.float32)
    return color_table, extinction_table


def shade_cells(vortex, color_table, extinction_table):
    position = (TF_POINTS - 1) * jax.nn.sigmoid(vortex_gain * vortex)
    color = jnp.zeros((3,) + vortex.shape, jnp.float32)
    extinction = jnp.zeros(vortex.shape, jnp.float32)
    for point in range(TF_POINTS):
        weight = jnp.maximum(0.0, 1.0 - jnp.abs(position - point))
        color = color + weight[None] * color_table[:, point].reshape(3, 1, 1, 1)
        extinction = extinction + weight * extinction_table[point]
    opacity = 1.0 - jnp.exp(-extinction)
    return color * opacity[None], opacity


def march_planes(color, opacity):
    def advance(carry, plane):
        accum, transmit = carry
        plane_color, plane_opacity = plane
        return (accum + transmit[None] * plane_color, transmit * (1.0 - plane_opacity)), None

    start = (jnp.zeros((3,) + opacity.shape[1:], jnp.float32), jnp.ones(opacity.shape[1:], jnp.float32))
    (accum, transmit), _ = lax.scan(advance, start, (jnp.moveaxis(color, 1, 0), opacity))
    return jnp.concatenate([accum, (1.0 - transmit)[None]], 0)


def reference(velocity, palette_color, palette_extinction, palette_index):
    gauss, deriv = filter_taps()
    color_table, extinction_table = lookup_tables(palette_color, palette_extinction, palette_index)
    padded_rows = jnp.pad(velocity, ((0, 0), (0, 0), (RADIUS, RADIUS), (0, 0)))
    zero_index = jnp.zeros((), jnp.int32)

    def render_block(start):
        block = lax.dynamic_slice(padded_rows, (zero_index, zero_index, start.astype(jnp.int32), zero_index), (3, NZ, 8 + 2 * RADIUS, NX))
        field = jnp.pad(block.astype(jnp.float32), ((0, 0), (RADIUS, RADIUS), (0, 0), (RADIUS, RADIUS)))
        smooth_x = smooth_along(field, gauss, 3)
        deriv_x = smooth_along(field, deriv, 3)
        grad_x = smooth_along(smooth_along(deriv_x, gauss, 2), gauss, 1)
        grad_y = smooth_along(smooth_along(smooth_x, deriv, 2), gauss, 1)
        grad_z = smooth_along(smooth_along(smooth_x, gauss, 2), deriv, 1)
        vortex = vortex_measure(grad_x, grad_y, grad_z)
        color, opacity = shade_cells(vortex, color_table, extinction_table)
        return march_planes(color, opacity)

    starts = jnp.arange(NY // 8, dtype=jnp.int32) * 8
    tiles = lax.map(render_block, starts)
    image = jnp.transpose(tiles, (1, 0, 2, 3)).reshape(4, NY, NX)
    return image.reshape(4, N_GY, CY, NX)
```

```python
import functools
import math

import jax
import jax.numpy as jnp
import numpy as np
from jax import lax
from jax.experimental import pallas as pl
from jax.experimental.pallas import tpu as pltpu
from jax.sharding import PartitionSpec as P

RADIUS = 4
TF_POINTS = 16
PAD = 8
BLOCK = 16
EDGE = 4
IN_FLIGHT = 3
MESH = pl.DeviceIdType.MESH

filter_sigma = 1.5
vortex_gain = 400.0


def filter_taps():
    weights = [
        math.exp(-((offset - RADIUS) ** 2) / (2.0 * filter_sigma**2))
        for offset in range(2 * RADIUS + 1)
    ]
    weight_sum = sum(weights)
    gauss = [weight / weight_sum for weight in weights]
    moment = sum(((offset - RADIUS) ** 2 * gauss[offset] for offset in range(2 * RADIUS + 1)))
    deriv = [(offset - RADIUS) * gauss[offset] / moment for offset in range(2 * RADIUS + 1)]
    return (gauss, deriv)


def banded(taps, outs, ins, shift):
    band = np.zeros((outs, ins), np.float64)
    for i in range(outs):
        for offset in range(2 * RADIUS + 1):
            k = i + shift + offset - RADIUS
            if 0 <= k < ins:
                band[i, k] = taps[offset]
    return band


def high_low(band):
    band = band.astype(np.float32)
    high = band.astype(jnp.bfloat16)
    low = (band - high.astype(np.float32)).astype(jnp.bfloat16)
    return high, low


def operators(half, columns):
    gauss, deriv = filter_taps()
    z_of = [banded(taps, half, half + 2 * RADIUS, RADIUS) for taps in (gauss, deriv)]
    y_of = [banded(taps, BLOCK, BLOCK + 2 * PAD, PAD) for taps in (gauss, deriv)]
    both = np.concatenate([np.kron(z_of[0], y_of[0]), np.kron(z_of[0], y_of[1]), np.kron(z_of[1], y_of[0])], 0)
    depth_rows = np.concatenate(high_low(both), 0)
    across = []
    for taps in (deriv, gauss):
        high, low = high_low(banded(taps, columns, columns, 0).T)
        across.append(np.block([[high, low], [high, np.zeros_like(low)]]))
    return depth_rows, np.stack(across)


def transfers(rows, n_gy):
    blocks = rows // BLOCK
    ends = [min(rows, (block + 1) * BLOCK + PAD) for block in range(blocks)]
    edges = [(1, rows - EDGE, PAD - EDGE, EDGE, 0), (-1, 0, PAD + rows, EDGE, blocks - 1)] if n_gy > 1 else []
    sides = [(1, rows - PAD, 0, PAD, 0), (-1, 0, PAD + rows, PAD, blocks - 1)] if n_gy > 1 else []
    moves = [(0, *side) for side in sides]
    for dz in (1, -1):
        start = 0
        for block, end in enumerate(ends):
            moves += [(dz, *edge) for edge in edges if edge[-1] == block]
            if end > start:
                moves.append((dz, 0, start, PAD + start, end - start, block))
            start = end
    return moves


def kernel(
    n, n_gy, velocity, depth_hbm, across_hbm, color_hbm, extinction_hbm, index_hbm, out,
    brick, depth_rows, across, color, extinction, index, table, front, staged, sent, got,
    local_sem, halo_send, halo_got, piece_send, piece_got, heard,
):
    parts, depth, rows, columns = velocity.shape
    half = depth // 2
    group = rows // n
    me, side = lax.axis_index("gz"), lax.axis_index("gy")
    has = {-1: {"gz": me > 0, "gy": side > 0}, 1: {"gz": me < n - 1, "gy": side < n_gy - 1}}
    moves = transfers(rows, n_gy)

    def present(dz, dy):
        flags = [has[d][axis] for d, axis in ((dz, "gz"), (dy, "gy")) if d != 0]
        return flags[0] if len(flags) == 1 else jnp.logical_and(flags[0], flags[1])

    def toward(dz, dy):
        return {"gz": me + dz, "gy": side + dy}

    barrier = pltpu.get_barrier_semaphore()
    expected = n.bit_length() - 1 + has[-1]["gz"].astype(jnp.int32) + has[1]["gz"].astype(jnp.int32)
    for dz, dy in [(dz, dy) for dz in (-1, 0, 1) for dy in (-1, 1) if n_gy > 1]:
        @pl.when(present(dz, dy))
        def _():
            pl.semaphore_signal(barrier, inc=1, device_id=toward(dz, dy), device_id_type=MESH)
        expected = expected + present(dz, dy).astype(jnp.int32)
    rounds = n.bit_length() - 1
    near = [jnp.bitwise_xor(me, 1 << level) for level in range(rounds)]
    for other in near:
        pl.semaphore_signal(barrier, inc=1, device_id={"gz": other, "gy": side}, device_id_type=MESH)
    for dz in (-1, 1):
        @pl.when(has[dz]["gz"])
        def _():
            pl.semaphore_signal(barrier, inc=1, device_id={"gz": me + dz, "gy": side}, device_id_type=MESH)

    def spread(level):
        if level > 0:
            pl.semaphore_wait(heard.at[level - 1], 1)
        if level < rounds:
            pl.semaphore_signal(
                heard.at[level], inc=1, device_id={"gz": near[level], "gy": side}, device_id_type=MESH
            )

    own = [
        pltpu.make_async_copy(source, target, local_sem.at[slot])
        for slot, (source, target) in enumerate(
            [
                (velocity, brick.at[:, pl.ds(RADIUS, depth), pl.ds(PAD, rows)]),
                (depth_hbm, depth_rows),
                (across_hbm, across),
                (color_hbm, color),
                (extinction_hbm, extinction),
                (index_hbm, index),
            ]
        )
    ]
    for copy in own:
        copy.start()
    for dz, at in ((-1, 0), (1, RADIUS + depth)):
        @pl.when(jnp.logical_not(has[dz]["gz"]))
        def _():
            brick[:, pl.ds(at, RADIUS)] = jnp.zeros((parts, RADIUS, rows + 2 * PAD, columns), brick.dtype)
    for dy, at in ((-1, 0), (1, PAD + rows)):
        @pl.when(jnp.logical_not(has[dy]["gy"]))
        def _():
            brick[:, :, pl.ds(at, PAD)] = jnp.zeros((parts, depth + 2 * RADIUS, PAD, columns), brick.dtype)
        if EDGE < PAD:
            spare = at if dy < 0 else at + EDGE
            for z_at in (0, RADIUS + depth):
                @pl.when(has[dy]["gy"])
                def _():
                    brick[:, pl.ds(z_at, RADIUS), pl.ds(spare, PAD - EDGE)] = jnp.zeros(
                        (parts, RADIUS, PAD - EDGE, columns), brick.dtype
                    )

    def halo(slot):
        dz, dy, y_from, y_to, count, _ = moves[slot]
        z_from = {-1: pl.ds(0, RADIUS), 0: pl.ds(0, depth), 1: pl.ds(depth - RADIUS, RADIUS)}[dz]
        z_to = {-1: pl.ds(RADIUS + depth, RADIUS), 0: pl.ds(RADIUS, depth), 1: pl.ds(0, RADIUS)}[dz]
        return pltpu.make_async_remote_copy(
            src_ref=velocity.at[:, z_from, pl.ds(y_from, count)],
            dst_ref=brick.at[:, z_to, pl.ds(y_to, count)],
            send_sem=halo_send.at[slot],
            recv_sem=halo_got.at[slot],
            device_id=toward(dz, dy),
            device_id_type=MESH,
        )

    queue = [(dz, block) for dz in (1, -1) for block in range(rows // BLOCK)]

    def each(dz, block, act):
        for slot, (slot_dz, slot_dy, _, _, _, needed) in enumerate(moves):
            if slot_dz == dz and block in (None, needed):
                @pl.when(present(slot_dz, slot_dy))
                def _():
                    act(halo(slot))

    def advance(step):
        each(*queue[step], lambda copy: copy.wait_send())
        if step + IN_FLIGHT < len(queue):
            each(*queue[step + IN_FLIGHT], lambda copy: copy.start())

    pl.semaphore_wait(barrier, expected)
    for entry in queue[:IN_FLIGHT]:
        each(*entry, lambda copy: copy.start())
    each(0, None, lambda copy: copy.start())
    spread(0)

    for copy in own:
        copy.wait()
    for channel in range(4):
        before = None
        for point in range(TF_POINTS):
            entry = index[point]
            value = color[channel, entry] if channel < 3 else extinction[entry]
            table[channel * TF_POINTS + point] = jnp.full((8, columns), value if point == 0 else value - before, jnp.float32)
            before = value

    def arrived(dz, block):
        for slot, (slot_dz, slot_dy, _, _, _, needed) in enumerate(moves):
            if needed == block and (slot_dz == dz or (slot_dz == 0 and dz == 1)):
                @pl.when(present(-slot_dz, -slot_dy))
                def _():
                    halo(slot).wait_recv()

    def piece(target):
        return pltpu.make_async_remote_copy(
            src_ref=sent.at[target],
            dst_ref=got.at[me],
            send_sem=piece_send.at[target],
            recv_sem=piece_got.at[me],
            device_id={"gz": target, "gy": side},
            device_id_type=MESH,
        )

    def filtered(values, band):
        high = values.astype(jnp.bfloat16)
        low = (values - high.astype(jnp.float32)).astype(jnp.bfloat16)
        both = jnp.dot(jnp.concatenate([high, low], 1), band, preferred_element_type=jnp.float32)
        return both[:, :columns] + both[:, columns:]

    span = half * BLOCK

    def march(block, first_plane, accum, transmit):
        window = jnp.concatenate(
            [
                brick[
                    c, pl.ds(first_plane, half + 2 * RADIUS), pl.ds(block * BLOCK, BLOCK + 2 * PAD), :
                ].reshape(-1, columns)
                for c in range(parts)
            ],
            1,
        )
        both = jnp.dot(depth_rows[...], window, preferred_element_type=jnp.float32)
        smooth = both[: 3 * span] + both[3 * span :]
        grads = []
        for c in range(parts):
            lanes = slice(c * columns, (c + 1) * columns)
            along_x = filtered(smooth[:span, lanes], across[0])
            others = filtered(smooth[span:, lanes], across[1])
            grads.append([along_x, others[:span], others[span:]])
        total = grads[0][0] * grads[0][0] + grads[1][1] * grads[1][1] + grads[2][2] * grads[2][2]
        cross = grads[0][1] * grads[1][0] + grads[0][2] * grads[2][0] + grads[1][2] * grads[2][1]
        vortex = -0.5 * total - cross
        position = (TF_POINTS - 1) * jax.nn.sigmoid(vortex_gain * vortex)
        position = position.reshape(half, BLOCK // 8, 8, columns)
        for plane in range(half):
            here = position[plane]
            looked = [jnp.broadcast_to(table[ch * TF_POINTS][None], here.shape) for ch in range(4)]
            for point in range(1, TF_POINTS):
                weight = jnp.clip(here - (point - 1), 0.0, 1.0)
                for ch in range(4):
                    looked[ch] = looked[ch] + weight * table[ch * TF_POINTS + point][None]
            passed = jnp.exp(-looked[3])
            share = transmit * (1.0 - passed)
            accum = [accum[ch] + share * looked[ch] for ch in range(3)]
            transmit = transmit * passed
        return accum, transmit

    shape = (BLOCK // 8, 8, columns)
    for block in range(rows // BLOCK):
        advance(block)
        arrived(1, block)
        if 0 < block <= rounds:
            spread(block)
        accum, transmit = march(block, 0, [jnp.zeros(shape, jnp.float32)] * 3, jnp.ones(shape, jnp.float32))
        for ch in range(3):
            front[block, ch] = accum[ch]
        front[block, 3] = transmit
    for block in range(rows // BLOCK):
        advance(rows // BLOCK + block)
        arrived(-1, block)
        accum, transmit = march(block, half, [front[block, ch] for ch in range(3)], front[block, 3])
        if block == 0:
            for level in range(rows // BLOCK, rounds + 1):
                spread(level)
        image = [part.reshape(BLOCK, columns) for part in accum + [1.0 - transmit]]
        for local in range(BLOCK // group):
            target = block * (BLOCK // group) + local
            for ch in range(4):
                staged[target, pl.ds(ch * group, group), :] = image[ch][local * group : (local + 1) * group]
            slab = staged[target].astype(jnp.bfloat16)

            @pl.when(me == target)
            def _():
                got[target] = slab

            @pl.when(me != target)
            def _():
                sent[target] = slab
                piece(target).start()

    for source in range(n):
        @pl.when(me != source)
        def _():
            pltpu.make_async_remote_copy(
                src_ref=sent.at[source],
                dst_ref=got.at[source],
                send_sem=piece_send.at[source],
                recv_sem=piece_got.at[source],
                device_id={"gz": source, "gy": side},
                device_id_type=MESH,
            ).wait_recv()
    accum = [jnp.zeros((group, columns), jnp.float32) for _ in range(3)]
    transmit = jnp.ones((group, columns), jnp.float32)
    for source in range(n):
        part = got[source].astype(jnp.float32)
        for ch in range(3):
            accum[ch] = accum[ch] + transmit * part[ch * group : (ch + 1) * group]
        transmit = transmit * (1.0 - part[3 * group :])
    for ch in range(3):
        out[ch, 0] = accum[ch]
    out[3, 0] = 1.0 - transmit

    for target in range(n):
        @pl.when(me != target)
        def _():
            piece(target).wait_send()
    each(0, None, lambda copy: copy.wait_send())


def solution(mesh):
    n, n_gy = mesh.shape["gz"], mesh.shape["gy"]

    def shards(velocity, palette_color, palette_extinction, palette_index):
        parts, depth, rows, columns = velocity.shape
        group = rows // n
        depth_rows, across = operators(depth // 2, columns)
        halos = len(transfers(rows, n_gy))
        return pl.pallas_call(
            functools.partial(kernel, n, n_gy),
            out_shape=pltpu.VMEM((4, 1, group, columns), jnp.float32),
            in_specs=[pl.BlockSpec(memory_space=pl.ANY)] * 6,
            out_specs=pl.BlockSpec(memory_space=pltpu.VMEM),
            scratch_shapes=[
                pltpu.VMEM((parts, depth + 2 * RADIUS, rows + 2 * PAD, columns), velocity.dtype),
                pltpu.VMEM(depth_rows.shape, jnp.bfloat16),
                pltpu.VMEM(across.shape, jnp.bfloat16),
                pltpu.SMEM(palette_color.shape, jnp.float32),
                pltpu.SMEM(palette_extinction.shape, jnp.float32),
                pltpu.SMEM(palette_index.shape, jnp.int32),
                pltpu.VMEM((4 * TF_POINTS, 8, columns), jnp.float32),
                pltpu.VMEM((rows // BLOCK, 4, BLOCK // 8, 8, columns), jnp.float32),
                pltpu.VMEM((n, 4 * group, columns), jnp.float32),
                pltpu.VMEM((n, 4 * group, columns), jnp.bfloat16),
                pltpu.VMEM((n, 4 * group, columns), jnp.bfloat16),
                pltpu.SemaphoreType.DMA((6,)),
                pltpu.SemaphoreType.DMA((halos,)),
                pltpu.SemaphoreType.DMA((halos,)),
                pltpu.SemaphoreType.DMA((n,)),
                pltpu.SemaphoreType.DMA((n,)),
                pltpu.SemaphoreType.REGULAR((n.bit_length() - 1,)),
            ],
            compiler_params=pltpu.CompilerParams(collective_id=0, has_side_effects=True),
        )(velocity, jnp.asarray(depth_rows), jnp.asarray(across), palette_color, palette_extinction, palette_index)

    return jax.shard_map(
        shards,
        mesh=mesh,
        in_specs=(P(None, "gz", "gy", None), P(), P(), P()),
        out_specs=P(None, "gy", "gz", None),
        check_vma=False,
    )
```

```python
import functools
import math

import jax
import jax.numpy as jnp
import numpy as np
from jax import lax
from jax.experimental import pallas as pl
from jax.experimental.pallas import tpu as pltpu
from jax.sharding import PartitionSpec as P

RADIUS = 4
TF_POINTS = 16
SUB = 8
BLOCK = 16
PLANE = 4
IN_FLIGHT = 3
MESH = pl.DeviceIdType.MESH
FAR, NEAR, LEVEL = 0, 1, 2

filter_sigma = 1.5
vortex_gain = 400.0


def filter_taps():
    weights = [
        math.exp(-((offset - RADIUS) ** 2) / (2.0 * filter_sigma**2))
        for offset in range(2 * RADIUS + 1)
    ]
    weight_sum = sum(weights)
    gauss = [weight / weight_sum for weight in weights]
    moment = sum(((offset - RADIUS) ** 2 * gauss[offset] for offset in range(2 * RADIUS + 1)))
    deriv = [(offset - RADIUS) * gauss[offset] / moment for offset in range(2 * RADIUS + 1)]
    return (gauss, deriv)


def banded(taps, outs, ins, shift):
    band = np.zeros((outs, ins), np.float64)
    for i in range(outs):
        for offset in range(2 * RADIUS + 1):
            k = i + shift + offset - RADIUS
            if 0 <= k < ins:
                band[i, k] = taps[offset]
    return band


def high_low(band):
    band = band.astype(np.float32)
    high = band.astype(jnp.bfloat16)
    low = (band - high.astype(np.float32)).astype(jnp.bfloat16)
    return high, low


def operators(half, columns):
    gauss, deriv = filter_taps()
    z_of = [banded(taps, half, half + 2 * RADIUS, RADIUS) for taps in (gauss, deriv)]
    y_of = [banded(taps, SUB, SUB + 2 * RADIUS, RADIUS) for taps in (gauss, deriv)]
    both = np.concatenate([np.kron(z_of[0], y_of[0]), np.kron(z_of[0], y_of[1]), np.kron(z_of[1], y_of[0])], 0)
    depth_rows = np.concatenate(high_low(both), 0)
    across = []
    for taps in (deriv, gauss):
        high, low = high_low(banded(taps, columns, columns, 0).T)
        across.append(np.block([[high, low], [high, np.zeros_like(low)]]))
    return depth_rows, np.stack(across)


def steps(rows):
    blocks = rows // BLOCK
    order = [(kind, block) for block in range(blocks) for kind in (FAR, NEAR)]
    if blocks > 1:
        order[-4:] = [(FAR, blocks - 2), (FAR, blocks - 1), (NEAR, blocks - 2), (NEAR, blocks - 1)]
    return order


def transfers(rows, n_gy):
    blocks = rows // BLOCK
    ends = [min(rows, (block + 1) * BLOCK + SUB) for block in range(blocks)]
    edges = [(1, rows - RADIUS, 0, RADIUS, 0), (-1, 0, RADIUS + rows, RADIUS, blocks - 1)] if n_gy > 1 else []
    moves = [(LEVEL, *edge) for edge in edges]
    for kind in (FAR, NEAR):
        start = 0
        for block, end in enumerate(ends):
            moves += [(kind, *edge) for edge in edges if edge[-1] == block]
            if end > start:
                moves.append((kind, 0, start, RADIUS + start, end - start, block))
            start = end
    return moves


def kernel(
    n, n_gy, velocity, depth_hbm, across_hbm, color_hbm, extinction_hbm, index_hbm, out,
    brick, depth_rows, across, color, extinction, index, table, staged, sent, got,
    local_sem, halo_send, halo_got, piece_send, piece_got, heard,
):
    parts, depth, rows, columns = velocity.shape
    half = depth // 2
    group = rows // n
    layers = n // PLANE
    me, side = lax.axis_index("gz"), lax.axis_index("gy")
    odd = lax.rem(me, 2)
    layer = me // PLANE
    near, far = me + 1 - 2 * odd, me - 1 + 2 * odd
    has_far = jnp.logical_and(far >= 0, far < n)
    has_row = {-1: side > 0, 1: side < n_gy - 1}
    has_layer = {-1: layer > 0, 1: layer < layers - 1}
    moves = transfers(rows, n_gy)
    order = steps(rows)
    row_ways = (-1, 1) if n_gy > 1 else ()

    def present(kind, dy):
        flags = ([has_far] if kind == FAR else []) + ([has_row[dy]] if dy else [])
        if not flags:
            return None
        return flags[0] if len(flags) == 1 else jnp.logical_and(flags[0], flags[1])

    def only(flag, act):
        if flag is None:
            act()
        else:
            pl.when(flag)(act)

    def toward(kind, dy):
        return {"gz": {FAR: far, NEAR: near, LEVEL: me}[kind], "gy": side + dy}

    own = [
        pltpu.make_async_copy(source, target, local_sem.at[slot])
        for slot, (source, target) in enumerate(
            [
                (velocity, brick.at[:, pl.ds(RADIUS, depth), pl.ds(RADIUS, rows)]),
                (depth_hbm, depth_rows),
                (across_hbm, across),
                (color_hbm, color),
                (extinction_hbm, extinction),
                (index_hbm, index),
            ]
        )
    ]

    barrier = pltpu.get_barrier_semaphore()
    expected = jnp.int32(0)
    greeted = [(toward(kind, dy), present(kind, dy)) for kind in (FAR, NEAR, LEVEL) for dy in (0, *row_ways) if kind != LEVEL or dy]
    greeted.append(({"gz": jnp.bitwise_xor(me, 2), "gy": side}, None))
    greeted += [({"gz": me + PLANE * way, "gy": side}, has_layer[way]) for way in (-1, 1)]
    for target, flag in greeted:
        def greet(target=target):
            pl.semaphore_signal(barrier, inc=1, device_id=target, device_id_type=MESH)
        only(flag, greet)
        expected = expected + (1 if flag is None else flag.astype(jnp.int32))

    for copy in own:
        copy.start()

    @pl.when(jnp.logical_not(has_far))
    def _():
        brick[:, pl.ds(odd * (RADIUS + depth), RADIUS)] = jnp.zeros((parts, RADIUS, rows + 2 * RADIUS, columns), brick.dtype)
    for dy, at in ((-1, 0), (1, RADIUS + rows)):
        @pl.when(jnp.logical_not(has_row[dy]))
        def _():
            brick[:, :, pl.ds(at, RADIUS)] = jnp.zeros((parts, depth + 2 * RADIUS, RADIUS, columns), brick.dtype)

    def halo(slot):
        kind, dy, y_from, y_to, count, _ = moves[slot]
        up = {FAR: odd, NEAR: 1 - odd, LEVEL: None}[kind]
        if kind == LEVEL:
            z_from, z_to = pl.ds(0, depth), pl.ds(RADIUS, depth)
        else:
            z_from, z_to = pl.ds(up * (depth - RADIUS), RADIUS), pl.ds((1 - up) * (RADIUS + depth), RADIUS)
        return pltpu.make_async_remote_copy(
            src_ref=velocity.at[:, z_from, pl.ds(y_from, count)],
            dst_ref=brick.at[:, z_to, pl.ds(y_to, count)],
            send_sem=halo_send.at[slot],
            recv_sem=halo_got.at[slot],
            device_id=toward(kind, dy),
            device_id_type=MESH,
        )

    def each(kind, block, act):
        for slot, (slot_kind, slot_dy, _, _, _, needed) in enumerate(moves):
            if slot_kind == kind and block in (None, needed):
                only(present(slot_kind, slot_dy), functools.partial(act, slot))

    def launch(slot):
        halo(slot).start()

    def advance(step):
        each(*order[step], lambda slot: halo(slot).wait_send())
        if step + IN_FLIGHT < len(order):
            each(*order[step + IN_FLIGHT], launch)

    def arrived(kind, block, level):
        for slot, (slot_kind, slot_dy, _, _, _, needed) in enumerate(moves):
            if needed == block and (slot_kind == kind or (slot_kind == LEVEL and level)):
                def take(slot=slot):
                    halo(slot).wait_recv()
                only(present(slot_kind, -slot_dy), take)

    pl.semaphore_wait(barrier, expected)
    for entry in order[:IN_FLIGHT]:
        each(*entry, launch)
    each(LEVEL, None, launch)

    def tell(slot, target):
        pl.semaphore_signal(heard.at[slot], inc=1, device_id={"gz": target, "gy": side}, device_id_type=MESH)

    def token(slot, came, target, goes):
        @pl.when(came)
        def _():
            pl.semaphore_wait(heard.at[slot], 1)

        @pl.when(goes)
        def _():
            tell(slot, target)

    tell(0, jnp.bitwise_xor(me, 1))
    pl.semaphore_wait(heard.at[0], 1)
    tell(1, jnp.bitwise_xor(me, 2))
    for copy in own[3:]:
        copy.wait()
    lane = lax.broadcasted_iota(jnp.int32, (SUB, columns), 1)
    for channel in range(4):
        values = []
        for point in range(TF_POINTS):
            entry = index[point]
            values.append(color[channel, entry] if channel < 3 else extinction[entry])
        level = jnp.zeros((SUB, columns), jnp.float32)
        slope = jnp.zeros((SUB, columns), jnp.float32)
        for point in range(TF_POINTS):
            level = jnp.where(lane == point, values[point], level)
            if point + 1 < TF_POINTS:
                slope = jnp.where(lane == point, values[point + 1] - values[point], slope)
        table[2 * channel] = level
        table[2 * channel + 1] = slope
    pl.semaphore_wait(heard.at[1], 1)
    token(2, has_layer[-1], me + PLANE, has_layer[1])
    token(3, has_layer[1], me - PLANE, has_layer[-1])
    for copy in own[:3]:
        copy.wait()

    def piece(target):
        return pltpu.make_async_remote_copy(
            src_ref=sent.at[target],
            dst_ref=got.at[me],
            send_sem=piece_send.at[target],
            recv_sem=piece_got.at[me],
            device_id={"gz": target, "gy": side},
            device_id_type=MESH,
        )

    def filtered(values, band):
        high = values.astype(jnp.bfloat16)
        low = (values - high.astype(jnp.float32)).astype(jnp.bfloat16)
        both = jnp.dot(jnp.concatenate([high, low], 1), band, preferred_element_type=jnp.float32)
        return both[:, :columns] + both[:, columns:]

    subs = BLOCK // SUB
    span = half * SUB

    def march(kind, block):
        upper = {FAR: odd, NEAR: 1 - odd}[kind]
        window = jnp.concatenate(
            [
                brick[
                    c, pl.ds(upper * half, half + 2 * RADIUS), pl.ds(block * BLOCK + sub * SUB, SUB + 2 * RADIUS), :
                ].reshape(-1, columns)
                for sub in range(subs)
                for c in range(parts)
            ],
            1,
        )
        both = jnp.dot(depth_rows[...], window, preferred_element_type=jnp.float32)
        smooth = both[: 3 * span] + both[3 * span :]
        cut = [smooth[:, at * columns : (at + 1) * columns] for at in range(subs * parts)]
        along_x = filtered(jnp.concatenate([one[:span] for one in cut], 0), across[0])
        others = filtered(jnp.concatenate([one[span:] for one in cut], 0), across[1])
        halves = []
        for sub in range(subs):
            grads = []
            for c in range(parts):
                at = sub * parts + c
                grads.append([
                    along_x[at * span : (at + 1) * span],
                    others[2 * at * span : (2 * at + 1) * span],
                    others[(2 * at + 1) * span : (2 * at + 2) * span],
                ])
            total = grads[0][0] * grads[0][0] + grads[1][1] * grads[1][1] + grads[2][2] * grads[2][2]
            cross = grads[0][1] * grads[1][0] + grads[0][2] * grads[2][0] + grads[1][2] * grads[2][1]
            vortex = -0.5 * total - cross
            position = (TF_POINTS - 1) * jax.nn.sigmoid(vortex_gain * vortex)
            accum, transmit = None, None
            for plane in range(half):
                here = position[plane * SUB : (plane + 1) * SUB]
                point = here.astype(jnp.int32)
                past = here - point.astype(jnp.float32)
                looked = [
                    jnp.take_along_axis(table[2 * ch], point, axis=1, mode="promise_in_bounds")
                    + past * jnp.take_along_axis(table[2 * ch + 1], point, axis=1, mode="promise_in_bounds")
                    for ch in range(4)
                ]
                passed = jnp.exp(-looked[3])
                if plane == 0:
                    share = 1.0 - passed
                    accum, transmit = [share * looked[ch] for ch in range(3)], passed
                else:
                    share = transmit * (1.0 - passed)
                    accum = [accum[ch] + share * looked[ch] for ch in range(3)]
                    transmit = transmit * passed
            halves.append(accum + [transmit])
        return [jnp.concatenate([part[ch] for part in halves], 0) for ch in range(4)]

    done = {}
    for step, (kind, block) in enumerate(order):
        advance(step)
        arrived(kind, block, (NEAR, block) not in done and (FAR, block) not in done)
        done[kind, block] = march(kind, block)
        if (1 - kind, block) not in done:
            continue
        first = [jnp.where(odd == 0, done[FAR, block][ch], done[NEAR, block][ch]) for ch in range(4)]
        then = [jnp.where(odd == 0, done[NEAR, block][ch], done[FAR, block][ch]) for ch in range(4)]
        image = [first[ch] + first[3] * then[ch] for ch in range(3)] + [1.0 - first[3] * then[3]]
        for local in range(BLOCK // group):
            target = block * (BLOCK // group) + local
            for ch in range(4):
                staged[target, pl.ds(ch * group, group), :] = image[ch][local * group : (local + 1) * group]
            slab = staged[target].astype(jnp.bfloat16)

            @pl.when(me == target)
            def _():
                got[target] = slab

            @pl.when(me != target)
            def _():
                sent[target] = slab
                piece(target).start()

    accum = [jnp.zeros((group, columns), jnp.float32) for _ in range(3)]
    transmit = jnp.ones((group, columns), jnp.float32)
    for source in range(n):
        @pl.when(me != source)
        def _():
            pltpu.make_async_remote_copy(
                src_ref=sent.at[source],
                dst_ref=got.at[source],
                send_sem=piece_send.at[source],
                recv_sem=piece_got.at[source],
                device_id={"gz": source, "gy": side},
                device_id_type=MESH,
            ).wait_recv()
    for source in range(n):
        part = got[source].astype(jnp.float32)
        for ch in range(3):
            accum[ch] = accum[ch] + transmit * part[ch * group : (ch + 1) * group]
        transmit = transmit * (1.0 - part[3 * group :])
    for ch in range(3):
        out[ch, 0] = accum[ch]
    out[3, 0] = 1.0 - transmit

    for target in range(n):
        @pl.when(me != target)
        def _():
            piece(target).wait_send()
    each(LEVEL, None, lambda slot: halo(slot).wait_send())


def solution(mesh):
    n, n_gy = mesh.shape["gz"], mesh.shape["gy"]

    def shards(velocity, palette_color, palette_extinction, palette_index):
        parts, depth, rows, columns = velocity.shape
        group = rows // n
        depth_rows, across = operators(depth // 2, columns)
        halos = len(transfers(rows, n_gy))
        return pl.pallas_call(
            functools.partial(kernel, n, n_gy),
            out_shape=pltpu.VMEM((4, 1, group, columns), jnp.float32),
            in_specs=[pl.BlockSpec(memory_space=pl.ANY)] * 6,
            out_specs=pl.BlockSpec(memory_space=pltpu.VMEM),
            scratch_shapes=[
                pltpu.VMEM((parts, depth + 2 * RADIUS, rows + 2 * RADIUS, columns), velocity.dtype),
                pltpu.VMEM(depth_rows.shape, jnp.bfloat16),
                pltpu.VMEM(across.shape, jnp.bfloat16),
                pltpu.SMEM(palette_color.shape, jnp.float32),
                pltpu.SMEM(palette_extinction.shape, jnp.float32),
                pltpu.SMEM(palette_index.shape, jnp.int32),
                pltpu.VMEM((8, SUB, columns), jnp.float32),
                pltpu.VMEM((n, 4 * group, columns), jnp.float32),
                pltpu.VMEM((n, 4 * group, columns), jnp.bfloat16),
                pltpu.VMEM((n, 4 * group, columns), jnp.bfloat16),
                pltpu.SemaphoreType.DMA((6,)),
                pltpu.SemaphoreType.DMA((halos,)),
                pltpu.SemaphoreType.DMA((halos,)),
                pltpu.SemaphoreType.DMA((n,)),
                pltpu.SemaphoreType.DMA((n,)),
                pltpu.SemaphoreType.REGULAR((4,)),
            ],
            compiler_params=pltpu.CompilerParams(collective_id=0, has_side_effects=True),
        )(velocity, jnp.asarray(depth_rows), jnp.asarray(across), palette_color, palette_extinction, palette_index)

    return jax.shard_map(
        shards,
        mesh=mesh,
        in_specs=(P(None, "gz", "gy", None), P(), P(), P()),
        out_specs=P(None, "gy", "gz", None),
        check_vma=False,
    )
```

```python
import functools
import math

import jax
import jax.numpy as jnp
import numpy as np
from jax import lax
from jax.experimental import pallas as pl
from jax.experimental.pallas import tpu as pltpu
from jax.sharding import PartitionSpec as P

RADIUS = 4
TF_POINTS = 16
SUB = 8
BLOCK = 16
PLANE = 4
MESH = pl.DeviceIdType.MESH
FAR, NEAR, LEVEL = 0, 1, 2

filter_sigma = 1.5
vortex_gain = 400.0


def filter_taps():
    weights = [
        math.exp(-((offset - RADIUS) ** 2) / (2.0 * filter_sigma**2))
        for offset in range(2 * RADIUS + 1)
    ]
    weight_sum = sum(weights)
    gauss = [weight / weight_sum for weight in weights]
    moment = sum(((offset - RADIUS) ** 2 * gauss[offset] for offset in range(2 * RADIUS + 1)))
    deriv = [(offset - RADIUS) * gauss[offset] / moment for offset in range(2 * RADIUS + 1)]
    return (gauss, deriv)


def banded(taps, outs, ins, shift):
    band = np.zeros((outs, ins), np.float64)
    for i in range(outs):
        for offset in range(2 * RADIUS + 1):
            k = i + shift + offset - RADIUS
            if 0 <= k < ins:
                band[i, k] = taps[offset]
    return band


def high_low(band):
    band = band.astype(np.float32)
    high = band.astype(jnp.bfloat16)
    low = (band - high.astype(np.float32)).astype(jnp.bfloat16)
    return high, low


def operators(half, columns):
    gauss, deriv = filter_taps()
    z_of = [banded(taps, half, half + 2 * RADIUS, RADIUS) for taps in (gauss, deriv)]
    y_of = [banded(taps, SUB, SUB + 2 * RADIUS, RADIUS) for taps in (gauss, deriv)]
    both = np.concatenate([np.kron(z_of[0], y_of[0]), np.kron(z_of[0], y_of[1]), np.kron(z_of[1], y_of[0])], 0)
    depth_rows = np.concatenate(high_low(both), 0)
    across = []
    for taps in (deriv, gauss):
        high, low = high_low(banded(taps, columns, columns, 0).T)
        across.append(np.block([[high, low], [high, np.zeros_like(low)]]))
    return depth_rows, np.stack(across)


def steps(rows):
    blocks = rows // BLOCK
    order = [(kind, block) for block in range(blocks) for kind in (FAR, NEAR)]
    if blocks > 1:
        order[-4:] = [(FAR, blocks - 2), (FAR, blocks - 1), (NEAR, blocks - 2), (NEAR, blocks - 1)]
    return order


def transfers(rows, n_gy):
    blocks = rows // BLOCK
    ends = [min(rows, (block + 1) * BLOCK + SUB) for block in range(blocks)]
    edges = [(1, rows - RADIUS, 0, RADIUS, 0), (-1, 0, RADIUS + rows, RADIUS, blocks - 1)] if n_gy > 1 else []
    moves = [(LEVEL, *edge) for edge in edges]
    for kind in (FAR, NEAR):
        start = 0
        for block, end in enumerate(ends):
            moves += [(kind, *edge) for edge in edges if edge[-1] == block]
            if end > start:
                moves.append((kind, 0, start, RADIUS + start, end - start, block))
            start = end
    return moves


def kernel(
    n, n_gy, velocity, depth_hbm, across_hbm, color_hbm, extinction_hbm, index_hbm, out,
    brick, depth_rows, across, color, extinction, index, table, staged, sent, got,
    local_sem, halo_send, halo_got, piece_send, piece_got, heard,
):
    parts, depth, rows, columns = velocity.shape
    half = depth // 2
    group = rows // n
    layers = n // PLANE
    me, side = lax.axis_index("gz"), lax.axis_index("gy")
    odd = lax.rem(me, 2)
    layer = me // PLANE
    near, far = me + 1 - 2 * odd, me - 1 + 2 * odd
    has_far = jnp.logical_and(far >= 0, far < n)
    has_row = {-1: side > 0, 1: side < n_gy - 1}
    has_layer = {-1: layer > 0, 1: layer < layers - 1}
    moves = transfers(rows, n_gy)
    order = steps(rows)
    row_ways = (-1, 1) if n_gy > 1 else ()

    def present(kind, dy):
        flags = ([has_far] if kind == FAR else []) + ([has_row[dy]] if dy else [])
        if not flags:
            return None
        return flags[0] if len(flags) == 1 else jnp.logical_and(flags[0], flags[1])

    def only(flag, act):
        if flag is None:
            act()
        else:
            pl.when(flag)(act)

    def toward(kind, dy):
        return {"gz": {FAR: far, NEAR: near, LEVEL: me}[kind], "gy": side + dy}

    own = [
        pltpu.make_async_copy(source, target, local_sem.at[slot])
        for slot, (source, target) in enumerate(
            [
                (velocity, brick.at[:, pl.ds(RADIUS, depth), pl.ds(RADIUS, rows)]),
                (depth_hbm, depth_rows),
                (across_hbm, across),
                (color_hbm, color),
                (extinction_hbm, extinction),
                (index_hbm, index),
            ]
        )
    ]

    barrier = pltpu.get_barrier_semaphore()
    expected = jnp.int32(0)
    greeted = [(toward(kind, dy), present(kind, dy)) for kind in (FAR, NEAR, LEVEL) for dy in (0, *row_ways) if kind != LEVEL or dy]
    greeted.append(({"gz": jnp.bitwise_xor(me, 2), "gy": side}, None))
    greeted += [({"gz": me + PLANE * way, "gy": side}, has_layer[way]) for way in (-1, 1)]
    for target, flag in greeted:
        def greet(target=target):
            pl.semaphore_signal(barrier, inc=1, device_id=target, device_id_type=MESH)
        only(flag, greet)
        expected = expected + (1 if flag is None else flag.astype(jnp.int32))

    for copy in own:
        copy.start()

    @pl.when(jnp.logical_not(has_far))
    def _():
        brick[:, pl.ds(odd * (RADIUS + depth), RADIUS)] = jnp.zeros((parts, RADIUS, rows + 2 * RADIUS, columns), brick.dtype)
    for dy, at in ((-1, 0), (1, RADIUS + rows)):
        @pl.when(jnp.logical_not(has_row[dy]))
        def _():
            brick[:, :, pl.ds(at, RADIUS)] = jnp.zeros((parts, depth + 2 * RADIUS, RADIUS, columns), brick.dtype)

    def halo(slot):
        kind, dy, y_from, y_to, count, _ = moves[slot]
        up = {FAR: odd, NEAR: 1 - odd, LEVEL: None}[kind]
        if kind == LEVEL:
            z_from, z_to = pl.ds(0, depth), pl.ds(RADIUS, depth)
        else:
            z_from, z_to = pl.ds(up * (depth - RADIUS), RADIUS), pl.ds((1 - up) * (RADIUS + depth), RADIUS)
        return pltpu.make_async_remote_copy(
            src_ref=velocity.at[:, z_from, pl.ds(y_from, count)],
            dst_ref=brick.at[:, z_to, pl.ds(y_to, count)],
            send_sem=halo_send.at[slot],
            recv_sem=halo_got.at[slot],
            device_id=toward(kind, dy),
            device_id_type=MESH,
        )

    def each(kind, block, act):
        for slot, (slot_kind, slot_dy, _, _, _, needed) in enumerate(moves):
            if slot_kind == kind and block in (None, needed):
                only(present(slot_kind, slot_dy), functools.partial(act, slot))

    def launch(slot):
        halo(slot).start()

    def arrived(kind, block, level):
        for slot, (slot_kind, slot_dy, _, _, _, needed) in enumerate(moves):
            if needed == block and (slot_kind == kind or (slot_kind == LEVEL and level)):
                def take(slot=slot):
                    halo(slot).wait_recv()
                only(present(slot_kind, -slot_dy), take)

    pl.semaphore_wait(barrier, expected)
    first = me == 1

    @pl.when(first)
    def _():
        for kind, block in order:
            each(1 - kind, block, launch)

    @pl.when(jnp.logical_not(first))
    def _():
        for kind, block in order:
            each(kind, block, launch)

    each(LEVEL, None, launch)

    def tell(slot, target):
        pl.semaphore_signal(heard.at[slot], inc=1, device_id={"gz": target, "gy": side}, device_id_type=MESH)

    blocks = rows // BLOCK
    last_layer = [((block + 1) * BLOCK // group - 1) // PLANE for block in range(blocks)]
    done_at = [max(order.index((FAR, block)), order.index((NEAR, block))) for block in range(blocks)]

    @pl.when(has_layer[1])
    def _():
        pl.when(has_layer[-1])(lambda: pl.semaphore_wait(heard.at[0], 1))
        tell(0, me + PLANE)

    def down(distance):
        @pl.when(layer + distance < layers)
        def _():
            pl.semaphore_wait(heard.at[distance], 1)

        if distance + 1 < layers:
            @pl.when(jnp.logical_and(layer + distance < layers, has_layer[-1]))
            def _():
                tell(distance + 1, me - PLANE)

    reached = [-1, 0]

    def learn(step):
        goal = max([(step + 2) // 2] + [last_layer[block] for block in range(blocks) if done_at[block] <= step + 1])
        for distance in range(reached[1] + 1, min(goal, layers - 1) + 1):
            down(distance)
            reached[1] = distance
        for block in range(reached[0] + 1, blocks):
            if last_layer[block] <= reached[1]:
                tell(layers + block, near)
                reached[0] = block

    @pl.when(has_layer[-1])
    def _():
        tell(1, me - PLANE)
    for copy in own[3:]:
        copy.wait()
    lane = lax.broadcasted_iota(jnp.int32, (SUB, columns), 1)
    for channel in range(4):
        values = []
        for point in range(TF_POINTS):
            entry = index[point]
            values.append(color[channel, entry] if channel < 3 else extinction[entry])
        level = jnp.zeros((SUB, columns), jnp.float32)
        slope = jnp.zeros((SUB, columns), jnp.float32)
        for point in range(TF_POINTS):
            level = jnp.where(lane == point, values[point], level)
            if point + 1 < TF_POINTS:
                slope = jnp.where(lane == point, values[point + 1] - values[point], slope)
        table[2 * channel] = level
        table[2 * channel + 1] = slope
    for copy in own[:3]:
        copy.wait()

    @pl.when(jnp.logical_and(has_layer[-1], jnp.logical_not(has_layer[1])))
    def _():
        pl.semaphore_wait(heard.at[0], 1)

    def piece(target):
        return pltpu.make_async_remote_copy(
            src_ref=sent.at[target],
            dst_ref=got.at[me],
            send_sem=piece_send.at[target],
            recv_sem=piece_got.at[me],
            device_id={"gz": target, "gy": side},
            device_id_type=MESH,
        )

    def filtered(values, band):
        high = values.astype(jnp.bfloat16)
        low = (values - high.astype(jnp.float32)).astype(jnp.bfloat16)
        both = jnp.dot(jnp.concatenate([high, low], 1), band, preferred_element_type=jnp.float32)
        return both[:, :columns] + both[:, columns:]

    subs = BLOCK // SUB
    span = half * SUB

    def march(kind, block):
        upper = {FAR: odd, NEAR: 1 - odd}[kind]
        window = jnp.concatenate(
            [
                brick[
                    c, pl.ds(upper * half, half + 2 * RADIUS), pl.ds(block * BLOCK + sub * SUB, SUB + 2 * RADIUS), :
                ].reshape(-1, columns)
                for sub in range(subs)
                for c in range(parts)
            ],
            1,
        )
        both = jnp.dot(depth_rows[...], window, preferred_element_type=jnp.float32)
        smooth = both[: 3 * span] + both[3 * span :]
        cut = [smooth[:, at * columns : (at + 1) * columns] for at in range(subs * parts)]
        along_x = filtered(jnp.concatenate([one[:span] for one in cut], 0), across[0])
        others = filtered(jnp.concatenate([one[span:] for one in cut], 0), across[1])
        halves = []
        for sub in range(subs):
            grads = []
            for c in range(parts):
                at = sub * parts + c
                grads.append([
                    along_x[at * span : (at + 1) * span],
                    others[2 * at * span : (2 * at + 1) * span],
                    others[(2 * at + 1) * span : (2 * at + 2) * span],
                ])
            total = grads[0][0] * grads[0][0] + grads[1][1] * grads[1][1] + grads[2][2] * grads[2][2]
            cross = grads[0][1] * grads[1][0] + grads[0][2] * grads[2][0] + grads[1][2] * grads[2][1]
            vortex = -0.5 * total - cross
            position = (TF_POINTS - 1) * jax.nn.sigmoid(vortex_gain * vortex)
            accum, transmit = None, None
            for plane in range(half):
                here = position[plane * SUB : (plane + 1) * SUB]
                point = here.astype(jnp.int32)
                past = here - point.astype(jnp.float32)
                looked = [
                    jnp.take_along_axis(table[2 * ch], point, axis=1, mode="promise_in_bounds")
                    + past * jnp.take_along_axis(table[2 * ch + 1], point, axis=1, mode="promise_in_bounds")
                    for ch in range(4)
                ]
                passed = jnp.exp(-looked[3])
                if plane == 0:
                    share = 1.0 - passed
                    accum, transmit = [share * looked[ch] for ch in range(3)], passed
                else:
                    share = transmit * (1.0 - passed)
                    accum = [accum[ch] + share * looked[ch] for ch in range(3)]
                    transmit = transmit * passed
            halves.append(accum + [transmit])
        return [jnp.concatenate([part[ch] for part in halves], 0) for ch in range(4)]

    done = {}
    for step, (kind, block) in enumerate(order):
        arrived(kind, block, (NEAR, block) not in done and (FAR, block) not in done)
        done[kind, block] = march(kind, block)
        learn(step)
        if (1 - kind, block) not in done:
            continue
        pl.semaphore_wait(heard.at[layers + block], 1)
        front = [jnp.where(odd == 0, done[FAR, block][ch], done[NEAR, block][ch]) for ch in range(4)]
        back = [jnp.where(odd == 0, done[NEAR, block][ch], done[FAR, block][ch]) for ch in range(4)]
        image = [front[ch] + front[3] * back[ch] for ch in range(3)] + [1.0 - front[3] * back[3]]
        for local in range(BLOCK // group):
            target = block * (BLOCK // group) + local
            for ch in range(4):
                staged[target, pl.ds(ch * group, group), :] = image[ch][local * group : (local + 1) * group]
            slab = staged[target].astype(jnp.bfloat16)

            @pl.when(me == target)
            def _():
                got[target] = slab

            @pl.when(me != target)
            def _():
                sent[target] = slab
                piece(target).start()

    accum = [jnp.zeros((group, columns), jnp.float32) for _ in range(3)]
    transmit = jnp.ones((group, columns), jnp.float32)
    for source in range(n):
        @pl.when(me != source)
        def _():
            pltpu.make_async_remote_copy(
                src_ref=sent.at[source],
                dst_ref=got.at[source],
                send_sem=piece_send.at[source],
                recv_sem=piece_got.at[source],
                device_id={"gz": source, "gy": side},
                device_id_type=MESH,
            ).wait_recv()
    for source in range(n):
        part = got[source].astype(jnp.float32)
        for ch in range(3):
            accum[ch] = accum[ch] + transmit * part[ch * group : (ch + 1) * group]
        transmit = transmit * (1.0 - part[3 * group :])
    for ch in range(3):
        out[ch, 0] = accum[ch]
    out[3, 0] = 1.0 - transmit

    for target in range(n):
        @pl.when(me != target)
        def _():
            piece(target).wait_send()
    for kind in (FAR, NEAR, LEVEL):
        each(kind, None, lambda slot: halo(slot).wait_send())


def solution(mesh):
    n, n_gy = mesh.shape["gz"], mesh.shape["gy"]

    def shards(velocity, palette_color, palette_extinction, palette_index):
        parts, depth, rows, columns = velocity.shape
        group = rows // n
        depth_rows, across = operators(depth // 2, columns)
        halos = len(transfers(rows, n_gy))
        return pl.pallas_call(
            functools.partial(kernel, n, n_gy),
            out_shape=pltpu.VMEM((4, 1, group, columns), jnp.float32),
            in_specs=[pl.BlockSpec(memory_space=pl.ANY)] * 6,
            out_specs=pl.BlockSpec(memory_space=pltpu.VMEM),
            scratch_shapes=[
                pltpu.VMEM((parts, depth + 2 * RADIUS, rows + 2 * RADIUS, columns), velocity.dtype),
                pltpu.VMEM(depth_rows.shape, jnp.bfloat16),
                pltpu.VMEM(across.shape, jnp.bfloat16),
                pltpu.SMEM(palette_color.shape, jnp.float32),
                pltpu.SMEM(palette_extinction.shape, jnp.float32),
                pltpu.SMEM(palette_index.shape, jnp.int32),
                pltpu.VMEM((8, SUB, columns), jnp.float32),
                pltpu.VMEM((n, 4 * group, columns), jnp.float32),
                pltpu.VMEM((n, 4 * group, columns), jnp.bfloat16),
                pltpu.VMEM((n, 4 * group, columns), jnp.bfloat16),
                pltpu.SemaphoreType.DMA((6,)),
                pltpu.SemaphoreType.DMA((halos,)),
                pltpu.SemaphoreType.DMA((halos,)),
                pltpu.SemaphoreType.DMA((n,)),
                pltpu.SemaphoreType.DMA((n,)),
                pltpu.SemaphoreType.REGULAR((n // PLANE + rows // BLOCK,)),
            ],
            compiler_params=pltpu.CompilerParams(collective_id=0, has_side_effects=True),
        )(velocity, jnp.asarray(depth_rows), jnp.asarray(across), palette_color, palette_extinction, palette_index)

    return jax.shard_map(
        shards,
        mesh=mesh,
        in_specs=(P(None, "gz", "gy", None), P(), P(), P()),
        out_specs=P(None, "gy", "gz", None),
        check_vma=False,
    )
```

```python
import functools
import math

import jax
import jax.numpy as jnp
import numpy as np
from jax import lax
from jax.experimental import pallas as pl
from jax.experimental.pallas import tpu as pltpu
from jax.sharding import PartitionSpec as P

RADIUS = 4
TF_POINTS = 16
SUB = 8
BLOCK = 16
PLANE = 4
MESH = pl.DeviceIdType.MESH
FAR, NEAR, LEVEL = 0, 1, 2
EARLY = -1

filter_sigma = 1.5
vortex_gain = 400.0


def filter_taps():
    weights = [
        math.exp(-((offset - RADIUS) ** 2) / (2.0 * filter_sigma**2))
        for offset in range(2 * RADIUS + 1)
    ]
    weight_sum = sum(weights)
    gauss = [weight / weight_sum for weight in weights]
    moment = sum(((offset - RADIUS) ** 2 * gauss[offset] for offset in range(2 * RADIUS + 1)))
    deriv = [(offset - RADIUS) * gauss[offset] / moment for offset in range(2 * RADIUS + 1)]
    return (gauss, deriv)


def banded(taps, outs, ins, shift):
    band = np.zeros((outs, ins), np.float64)
    for i in range(outs):
        for offset in range(2 * RADIUS + 1):
            k = i + shift + offset - RADIUS
            if 0 <= k < ins:
                band[i, k] = taps[offset]
    return band


def high_low(band):
    band = band.astype(np.float32)
    high = band.astype(jnp.bfloat16)
    low = (band - high.astype(np.float32)).astype(jnp.bfloat16)
    return high, low


def operators(half, columns):
    gauss, deriv = filter_taps()
    z_of = [banded(taps, half, half + 2 * RADIUS, RADIUS) for taps in (gauss, deriv)]
    y_of = [banded(taps, SUB, SUB + 2 * RADIUS, RADIUS) for taps in (gauss, deriv)]
    both = np.concatenate([np.kron(z_of[0], y_of[0]), np.kron(z_of[0], y_of[1]), np.kron(z_of[1], y_of[0])], 0)
    depth_rows = np.concatenate(high_low(both), 0)
    across = []
    for taps in (deriv, gauss):
        high, low = high_low(banded(taps, columns, columns, 0).T)
        across.append(np.block([[high, low], [high, np.zeros_like(low)]]))
    return depth_rows, np.stack(across)


def steps(rows):
    blocks = rows // BLOCK
    order = [(kind, block) for block in range(blocks) for kind in (FAR, NEAR)]
    if blocks > 1:
        order[-4:] = [(FAR, blocks - 2), (FAR, blocks - 1), (NEAR, blocks - 2), (NEAR, blocks - 1)]
    return order


def transfers(rows, n_gy):
    blocks = rows // BLOCK
    top = rows - RADIUS if n_gy > 1 else rows
    ends = [min(top, (block + 1) * BLOCK + SUB) for block in range(blocks)]
    moves = []
    for kind in (FAR, NEAR):
        start = 0
        for block, end in enumerate(ends):
            if end > start:
                moves.append((kind, 0, start, RADIUS + start, end - start, block))
            start = end
    if n_gy > 1:
        moves += [(kind, 0, top, RADIUS + top, RADIUS, EARLY) for kind in (FAR, NEAR)]
        moves += [(kind, *edge) for kind in (LEVEL, FAR, NEAR) for edge in ((1, top, 0, RADIUS, 0), (-1, 0, RADIUS + rows, RADIUS, blocks - 1))]
    return moves


def kernel(
    n, n_gy, velocity, depth_hbm, across_hbm, color_hbm, extinction_hbm, index_hbm, out,
    brick, depth_rows, across, color, extinction, index, table, staged, sent, got,
    local_sem, halo_send, halo_got, piece_send, piece_got, heard,
):
    parts, depth, rows, columns = velocity.shape
    half = depth // 2
    group = rows // n
    layers = n // PLANE
    me, side = lax.axis_index("gz"), lax.axis_index("gy")
    odd = lax.rem(me, 2)
    layer = me // PLANE
    near, far = me + 1 - 2 * odd, me - 1 + 2 * odd
    has_far = jnp.logical_and(far >= 0, far < n)
    has_row = {-1: side > 0, 1: side < n_gy - 1}
    has_layer = {-1: layer > 0, 1: layer < layers - 1}
    moves = transfers(rows, n_gy)
    order = steps(rows)
    row_ways = (-1, 1) if n_gy > 1 else ()

    def present(kind, dy):
        flags = ([has_far] if kind == FAR else []) + ([has_row[dy]] if dy else [])
        if not flags:
            return None
        return flags[0] if len(flags) == 1 else jnp.logical_and(flags[0], flags[1])

    def only(flag, act):
        if flag is None:
            act()
        else:
            pl.when(flag)(act)

    def toward(kind, dy):
        return {"gz": {FAR: far, NEAR: near, LEVEL: me}[kind], "gy": side + dy}

    own = [
        pltpu.make_async_copy(source, target, local_sem.at[slot])
        for slot, (source, target) in enumerate(
            [
                (velocity, brick.at[:, pl.ds(RADIUS, depth), pl.ds(RADIUS, rows)]),
                (depth_hbm, depth_rows),
                (across_hbm, across),
                (color_hbm, color),
                (extinction_hbm, extinction),
                (index_hbm, index),
            ]
        )
    ]

    barrier = pltpu.get_barrier_semaphore()
    expected = jnp.int32(0)
    greeted = [(toward(kind, dy), present(kind, dy)) for kind, dy in [(FAR, 0), (NEAR, 0), *((LEVEL, way) for way in row_ways)]]
    greeted.append(({"gz": jnp.bitwise_xor(me, 2), "gy": side}, None))
    greeted += [({"gz": me + PLANE * way, "gy": side}, has_layer[way]) for way in (-1, 1)]
    for target, flag in greeted:
        def greet(target=target):
            pl.semaphore_signal(barrier, inc=1, device_id=target, device_id_type=MESH)
        only(flag, greet)
        expected = expected + (1 if flag is None else flag.astype(jnp.int32))

    for copy in own:
        copy.start()

    @pl.when(jnp.logical_not(has_far))
    def _():
        brick[:, pl.ds(odd * (RADIUS + depth), RADIUS)] = jnp.zeros((parts, RADIUS, rows + 2 * RADIUS, columns), brick.dtype)
    for dy, at in ((-1, 0), (1, RADIUS + rows)):
        @pl.when(jnp.logical_not(has_row[dy]))
        def _():
            brick[:, :, pl.ds(at, RADIUS)] = jnp.zeros((parts, depth + 2 * RADIUS, RADIUS, columns), brick.dtype)

    def halo(slot):
        kind, dy, y_from, y_to, count, _ = moves[slot]
        up = {FAR: odd, NEAR: 1 - odd, LEVEL: None}[kind]
        source, row_from = velocity, y_from
        if kind != LEVEL and dy:
            z_from = z_to = pl.ds({FAR: odd, NEAR: 1 - odd}[kind] * (RADIUS + depth), RADIUS)
            source, row_from = brick, RADIUS + y_from
        elif kind == LEVEL:
            z_from, z_to = pl.ds(0, depth), pl.ds(RADIUS, depth)
        else:
            z_from, z_to = pl.ds(up * (depth - RADIUS), RADIUS), pl.ds((1 - up) * (RADIUS + depth), RADIUS)
        return pltpu.make_async_remote_copy(
            src_ref=source.at[:, z_from, pl.ds(row_from, count)],
            dst_ref=brick.at[:, z_to, pl.ds(y_to, count)],
            send_sem=halo_send.at[slot],
            recv_sem=halo_got.at[slot],
            device_id=toward(LEVEL if dy else kind, dy),
            device_id_type=MESH,
        )

    def each(kind, block, act):
        for slot, (slot_kind, slot_dy, _, _, _, needed) in enumerate(moves):
            if slot_kind == kind and block in (None, needed) and (block is None or kind == LEVEL or slot_dy == 0):
                only(present(slot_kind, slot_dy), functools.partial(act, slot))

    def launch(slot):
        halo(slot).start()

    def arrived(kind, block, level):
        for slot, (slot_kind, slot_dy, _, _, _, needed) in sorted(enumerate(moves), key=lambda move: abs(move[1][1])):
            if needed == block and (slot_kind == kind or (slot_kind == LEVEL and level)):
                def take(slot=slot):
                    halo(slot).wait_recv()
                only(present(slot_kind, -slot_dy), take)

    pl.semaphore_wait(barrier, expected)
    def take(kind):
        each(kind, EARLY, lambda slot: halo(slot).wait_recv())

    def relay(kind, way):
        for slot, (slot_kind, slot_dy, *_) in enumerate(moves):
            if slot_kind == kind and slot_dy == way:
                only(present(kind, way), functools.partial(launch, slot))

    first = me == 1
    for kind in (FAR, NEAR):
        each(kind, EARLY, launch)

    @pl.when(first)
    def _():
        for kind, block in order:
            each(1 - kind, block, launch)

    @pl.when(jnp.logical_not(first))
    def _():
        for kind, block in order:
            each(kind, block, launch)

    each(LEVEL, None, launch)

    def tell(slot, target):
        pl.semaphore_signal(heard.at[slot], inc=1, device_id={"gz": target, "gy": side}, device_id_type=MESH)

    blocks = rows // BLOCK
    last_layer = [((block + 1) * BLOCK // group - 1) // PLANE for block in range(blocks)]
    done_at = [max(order.index((FAR, block)), order.index((NEAR, block))) for block in range(blocks)]

    @pl.when(has_layer[1])
    def _():
        pl.when(has_layer[-1])(lambda: pl.semaphore_wait(heard.at[0], 1))
        tell(0, me + PLANE)

    def down(distance):
        @pl.when(layer + distance < layers)
        def _():
            pl.semaphore_wait(heard.at[distance], 1)

        if distance + 1 < layers:
            @pl.when(jnp.logical_and(layer + distance < layers, has_layer[-1]))
            def _():
                tell(distance + 1, me - PLANE)

    reached = [-1, 0]

    def learn(step):
        goal = max([(step + 2) // 2] + [last_layer[block] for block in range(blocks) if done_at[block] <= step + 1])
        for distance in range(reached[1] + 1, min(goal, layers - 1) + 1):
            down(distance)
            reached[1] = distance
        for block in range(reached[0] + 1, blocks):
            if last_layer[block] <= reached[1]:
                tell(layers + block, near)
                reached[0] = block

    @pl.when(has_layer[-1])
    def _():
        tell(1, me - PLANE)
    for copy in own[3:]:
        copy.wait()
    lane = lax.broadcasted_iota(jnp.int32, (SUB, columns), 1)
    for channel in range(4):
        values = []
        for point in range(TF_POINTS):
            entry = index[point]
            values.append(color[channel, entry] if channel < 3 else extinction[entry])
        level = jnp.zeros((SUB, columns), jnp.float32)
        slope = jnp.zeros((SUB, columns), jnp.float32)
        for point in range(TF_POINTS):
            level = jnp.where(lane == point, values[point], level)
            if point + 1 < TF_POINTS:
                slope = jnp.where(lane == point, values[point + 1] - values[point], slope)
        table[2 * channel] = level
        table[2 * channel + 1] = slope
    for copy in own[:3]:
        copy.wait()

    @pl.when(jnp.logical_and(has_layer[-1], jnp.logical_not(has_layer[1])))
    def _():
        pl.semaphore_wait(heard.at[0], 1)

    def piece(target):
        return pltpu.make_async_remote_copy(
            src_ref=sent.at[target],
            dst_ref=got.at[me],
            send_sem=piece_send.at[target],
            recv_sem=piece_got.at[me],
            device_id={"gz": target, "gy": side},
            device_id_type=MESH,
        )

    def filtered(values, band):
        high = values.astype(jnp.bfloat16)
        low = (values - high.astype(jnp.float32)).astype(jnp.bfloat16)
        both = jnp.dot(jnp.concatenate([high, low], 1), band, preferred_element_type=jnp.float32)
        return both[:, :columns] + both[:, columns:]

    subs = BLOCK // SUB
    span = half * SUB

    def march(kind, block):
        upper = {FAR: odd, NEAR: 1 - odd}[kind]
        window = jnp.concatenate(
            [
                brick[
                    c, pl.ds(upper * half, half + 2 * RADIUS), pl.ds(block * BLOCK + sub * SUB, SUB + 2 * RADIUS), :
                ].reshape(-1, columns)
                for sub in range(subs)
                for c in range(parts)
            ],
            1,
        )
        both = jnp.dot(depth_rows[...], window, preferred_element_type=jnp.float32)
        smooth = both[: 3 * span] + both[3 * span :]
        cut = [smooth[:, at * columns : (at + 1) * columns] for at in range(subs * parts)]
        along_x = filtered(jnp.concatenate([one[:span] for one in cut], 0), across[0])
        others = filtered(jnp.concatenate([one[span:] for one in cut], 0), across[1])
        halves = []
        for sub in range(subs):
            grads = []
            for c in range(parts):
                at = sub * parts + c
                grads.append([
                    along_x[at * span : (at + 1) * span],
                    others[2 * at * span : (2 * at + 1) * span],
                    others[(2 * at + 1) * span : (2 * at + 2) * span],
                ])
            total = grads[0][0] * grads[0][0] + grads[1][1] * grads[1][1] + grads[2][2] * grads[2][2]
            cross = grads[0][1] * grads[1][0] + grads[0][2] * grads[2][0] + grads[1][2] * grads[2][1]
            vortex = -0.5 * total - cross
            position = (TF_POINTS - 1) * jax.nn.sigmoid(vortex_gain * vortex)
            accum, transmit = None, None
            for plane in range(half):
                here = position[plane * SUB : (plane + 1) * SUB]
                point = here.astype(jnp.int32)
                past = here - point.astype(jnp.float32)
                looked = [
                    jnp.take_along_axis(table[2 * ch], point, axis=1, mode="promise_in_bounds")
                    + past * jnp.take_along_axis(table[2 * ch + 1], point, axis=1, mode="promise_in_bounds")
                    for ch in range(4)
                ]
                passed = jnp.exp(-looked[3])
                if plane == 0:
                    share = 1.0 - passed
                    accum, transmit = [share * looked[ch] for ch in range(3)], passed
                else:
                    share = transmit * (1.0 - passed)
                    accum = [accum[ch] + share * looked[ch] for ch in range(3)]
                    transmit = transmit * passed
            halves.append(accum + [transmit])
        return [jnp.concatenate([part[ch] for part in halves], 0) for ch in range(4)]

    done = {}
    for step, (kind, block) in enumerate(order):
        if block == 0 and row_ways:
            take(kind)
            relay(kind, 1)
        arrived(kind, block, (NEAR, block) not in done and (FAR, block) not in done)
        if block == 0 and row_ways:
            relay(kind, -1)
        done[kind, block] = march(kind, block)
        learn(step)
        if (1 - kind, block) not in done:
            continue
        pl.semaphore_wait(heard.at[layers + block], 1)
        front = [jnp.where(odd == 0, done[FAR, block][ch], done[NEAR, block][ch]) for ch in range(4)]
        back = [jnp.where(odd == 0, done[NEAR, block][ch], done[FAR, block][ch]) for ch in range(4)]
        image = [front[ch] + front[3] * back[ch] for ch in range(3)] + [1.0 - front[3] * back[3]]
        for local in range(BLOCK // group):
            target = block * (BLOCK // group) + local
            for ch in range(4):
                staged[target, pl.ds(ch * group, group), :] = image[ch][local * group : (local + 1) * group]
            slab = staged[target].astype(jnp.bfloat16)

            @pl.when(me == target)
            def _():
                got[target] = slab

            @pl.when(me != target)
            def _():
                sent[target] = slab
                piece(target).start()

    accum = [jnp.zeros((group, columns), jnp.float32) for _ in range(3)]
    transmit = jnp.ones((group, columns), jnp.float32)
    for source in range(n):
        @pl.when(me != source)
        def _():
            pltpu.make_async_remote_copy(
                src_ref=sent.at[source],
                dst_ref=got.at[source],
                send_sem=piece_send.at[source],
                recv_sem=piece_got.at[source],
                device_id={"gz": source, "gy": side},
                device_id_type=MESH,
            ).wait_recv()
    for source in range(n):
        part = got[source].astype(jnp.float32)
        for ch in range(3):
            accum[ch] = accum[ch] + transmit * part[ch * group : (ch + 1) * group]
        transmit = transmit * (1.0 - part[3 * group :])
    for ch in range(3):
        out[ch, 0] = accum[ch]
    out[3, 0] = 1.0 - transmit

    for target in range(n):
        @pl.when(me != target)
        def _():
            piece(target).wait_send()
    for kind in (FAR, NEAR, LEVEL):
        each(kind, None, lambda slot: halo(slot).wait_send())


def solution(mesh):
    n, n_gy = mesh.shape["gz"], mesh.shape["gy"]

    def shards(velocity, palette_color, palette_extinction, palette_index):
        parts, depth, rows, columns = velocity.shape
        group = rows // n
        depth_rows, across = operators(depth // 2, columns)
        halos = len(transfers(rows, n_gy))
        return pl.pallas_call(
            functools.partial(kernel, n, n_gy),
            out_shape=pltpu.VMEM((4, 1, group, columns), jnp.float32),
            in_specs=[pl.BlockSpec(memory_space=pl.ANY)] * 6,
            out_specs=pl.BlockSpec(memory_space=pltpu.VMEM),
            scratch_shapes=[
                pltpu.VMEM((parts, depth + 2 * RADIUS, rows + 2 * RADIUS, columns), velocity.dtype),
                pltpu.VMEM(depth_rows.shape, jnp.bfloat16),
                pltpu.VMEM(across.shape, jnp.bfloat16),
                pltpu.SMEM(palette_color.shape, jnp.float32),
                pltpu.SMEM(palette_extinction.shape, jnp.float32),
                pltpu.SMEM(palette_index.shape, jnp.int32),
                pltpu.VMEM((8, SUB, columns), jnp.float32),
                pltpu.VMEM((n, 4 * group, columns), jnp.float32),
                pltpu.VMEM((n, 4 * group, columns), jnp.bfloat16),
                pltpu.VMEM((n, 4 * group, columns), jnp.bfloat16),
                pltpu.SemaphoreType.DMA((6,)),
                pltpu.SemaphoreType.DMA((halos,)),
                pltpu.SemaphoreType.DMA((halos,)),
                pltpu.SemaphoreType.DMA((n,)),
                pltpu.SemaphoreType.DMA((n,)),
                pltpu.SemaphoreType.REGULAR((n // PLANE + rows // BLOCK,)),
            ],
            compiler_params=pltpu.CompilerParams(collective_id=0, has_side_effects=True),
        )(velocity, jnp.asarray(depth_rows), jnp.asarray(across), palette_color, palette_extinction, palette_index)

    return jax.shard_map(
        shards,
        mesh=mesh,
        in_specs=(P(None, "gz", "gy", None), P(), P(), P()),
        out_specs=P(None, "gy", "gz", None),
        check_vma=False,
    )
```
